32 devices in a mesh: grp: 2 (over x), inp: 4 (over y, core), tm: 4 (over z).
Axes of the slice: x: 2, y: 2, z: 4, core: 2. Of those that a mesh axis runs over, the one named last changes fastest.
Arguments:
- samples: bfloat16 [64, 1024, 8192], P(('grp', 'tm'), 'inp'), parts along dimension 0, may hold values from -6 to 6
- fir: float32 [16, 8192], replicated, may hold values from -1 to 1
- flags: int32 [64, 1024], P(('grp', 'tm'), 'inp'), parts along dimension 0, may hold values 0 or 1
Outputs:
- visibilities: float32 [16, 2, 1024, 1024], P(('grp', 'tm'), None, 'inp'), parts along dimension 0
The draws below stay inside these ranges and needn't reach their ends.
There are 2 independent parts, one for each index of `grp`. The reference program is written for one: setup_inputs(seed, part) draws one part's arguments, and reference() takes and returns one part's arrays. A program takes and returns all parts, laid end to end along the dimension named above; an argument that names none is the same for every part. Nothing has to cross between parts.
All inputs are finite; a program needn't handle non-finite values. No bound on the sum of `flags` on one device may be relied on, other than what follows from the above.
Results may differ from the reference program's by a relative error of at most 0.0063.
Values may be sent and summed in bfloat16 or wider, within the bound.
A program may use at most 256 MiB of HBM per device.

```python
import math
import jax
import jax.numpy as jnp
from jax import lax

NI = 1024
NCH = 4096
LEN = 8192
TAPS = 16
SPEC_DEV = 8
NSPEC = 32
CB = 8
HOPS = 2


def touch_ends(values, rng, least, high):
    place = [jax.random.randint(jax.random.fold_in(rng, axis), (), 0, length) for axis, length in enumerate(values.shape)]
    widest = values.shape.index(max(values.shape))
    next_to = place[:widest] + [(place[widest] + 1) % values.shape[widest]] + place[widest + 1:]
    return values.at[tuple(place)].set(least).at[tuple(next_to)].set(high)


def level_of(rng, extent, pieces, smallest, high):
    loudness, own = 1.0, jax.random.fold_in(rng, 6)
    for dim, parts in pieces:
        steps = jnp.exp(jax.random.uniform(jax.random.fold_in(own, dim), (parts,), jnp.float32, smallest / len(pieces), high / len(pieces)))
        loudness = loudness * jnp.repeat(steps, extent[dim] // parts).reshape([-1 if axis == dim else 1 for axis in range(len(extent))])
    return loudness


def noise(rng, shape, spread, limit, pieces=(), kind=jnp.bfloat16):
    values = jax.random.normal(rng, shape, jnp.float32) * spread
    if len(pieces) > 0:
        values = level_of(rng, shape, pieces, -0.22, 0.18) * values
    return jnp.clip(values, min=-limit, max=limit).astype(kind)


def setup_inputs(seed: int = 0, part: int = 0) -> dict:
    splits = jax.random.split(jax.random.key(seed), 4)
    part_keys = jax.random.split(jax.random.fold_in(splits[3], part), 4)
    return {
        "samples": noise(part_keys[0], (NSPEC, NI, LEN), 1.0, 6.0, ((0, 4), (1, 4))),
        "fir": noise(splits[1], (TAPS, LEN), 0.25, 1.0, (), jnp.float32),
        "flags": touch_ends((jax.random.randint(part_keys[2], (NSPEC, NI), 0, 8) < 7).astype(jnp.int32), jax.random.fold_in(part_keys[2], 1), 0, 1),
    }


def band_table(length, count, lowest):
    sample_ids = jnp.arange(length, dtype=jnp.int32)
    channel_ids = lowest + jnp.arange(count, dtype=jnp.int32)
    phase = sample_ids[:, None] * channel_ids[None, :] % length
    angle = 2.0 * math.pi / length * phase.astype(jnp.float32)
    factor = math.sqrt(2.0 / length)
    both = jnp.concatenate([factor * jnp.cos(angle), -factor * jnp.sin(angle)], axis=1)
    return both.astype(jnp.bfloat16)

def reference(samples, fir, flags):
    block = min(NI, 128)
    table = band_table(LEN, CB, NCH // 4).astype(jnp.float32)
    frame_ids = jnp.arange(NSPEC, dtype=jnp.int32)
    own_block = frame_ids // SPEC_DEV

    def channelize(block_index):
        first = (block_index * block).astype(jnp.int32)
        frames = lax.dynamic_slice_in_dim(samples, first, block, 1)
        padded = jnp.concatenate([jnp.zeros((TAPS - 1, block, LEN), samples.dtype), frames], axis=0)
        band = jnp.zeros((NSPEC, block, 2 * CB), jnp.float32)
        for hop in range(HOPS + 1):
            filtered = jnp.zeros((NSPEC, block, LEN), jnp.float32)
            for tap_index in range(TAPS):
                source = frame_ids - TAPS + 1 + tap_index
                source_block = jnp.floor_divide(source, SPEC_DEV)
                keep = (own_block - source_block == hop).astype(jnp.float32)
                filtered = filtered + keep[:, None, None] * fir[tap_index][None, None, :] * padded[tap_index:tap_index + NSPEC].astype(jnp.float32)
            part = filtered.astype(jnp.bfloat16).astype(jnp.float32)
            band = band + jnp.einsum('kbl,lq->kbq', part, table, precision=lax.Precision.HIGHEST)
        good = lax.dynamic_slice_in_dim(flags, first, block, 1).astype(jnp.float32)
        return (band * good[:, :, None]).astype(jnp.bfloat16)
    blocks = lax.map(channelize, jnp.arange(NI // block, dtype=jnp.int32))
    spectra = jnp.transpose(blocks, (1, 0, 2, 3)).reshape(NSPEC, NI, 2, CB)
    spectra = jnp.transpose(spectra, (0, 2, 3, 1))

    def correlate(channel):
        column = lax.dynamic_index_in_dim(spectra, channel, 2, keepdims=False).astype(jnp.float32)
        rotated = jnp.stack([-column[:, 1], column[:, 0]], axis=1)
        real = jnp.einsum('kpi,kpj->ij', column, column, precision=lax.Precision.HIGHEST)
        imag = jnp.einsum('kpi,kpj->ij', column, rotated, precision=lax.Precision.HIGHEST)
        return jnp.stack([real, imag], axis=0) / NSPEC
    return lax.map(correlate, jnp.arange(CB, dtype=jnp.int32))
```

```python
import math

import jax
import jax.numpy as jnp
from jax import lax
from jax.sharding import PartitionSpec as P

NCH = 4096
CH_DEV = 2


def from_behind(value, axis, steps):
    count = lax.axis_size(axis)
    first, last = (max(0, -steps), min(count, count - steps))
    return lax.ppermute(value, axis, [(source, source + steps) for source in range(first, last)])


def band_table(length, count, lowest):
    sample_ids = jnp.arange(length, dtype=jnp.int32)
    channel_ids = lowest + jnp.arange(count, dtype=jnp.int32)
    phase = sample_ids[:, None] * channel_ids[None, :] % length
    angle = 2.0 * math.pi / length * phase.astype(jnp.float32)
    factor = math.sqrt(2.0 / length)
    both = jnp.concatenate([factor * jnp.cos(angle), -factor * jnp.sin(angle)], axis=1)
    return both.astype(jnp.bfloat16)


def correlate(own, piece):
    rotated = jnp.stack([-piece[:, 1], piece[:, 0]], axis=1)
    real = jnp.einsum("spci,spcj->cij", own, piece, preferred_element_type=jnp.float32)
    imag = jnp.einsum("spci,spcj->cij", own, rotated, preferred_element_type=jnp.float32)
    return jnp.stack([real, imag], axis=1) / own.shape[0]


def shards(samples, fir, flags):
    frame_count = samples.shape[0]
    inputs_here = samples.shape[1]
    taps = fir.shape[0]
    reach = (taps + frame_count - 2) // frame_count
    band_width = CH_DEV * lax.axis_size("tm")
    table = band_table(samples.shape[2], band_width, NCH // 4)
    table = table.astype(jnp.float32).T
    wide = table.shape[0]
    weights = (fir[::-1][:, None, :] * table[None]).astype(jnp.bfloat16)
    weights = weights.reshape(taps * wide, -1)
    products = lax.dot_general(samples, weights, (((2,), (1,)), ((), ())), preferred_element_type=jnp.float32)
    blocks = reach + 1
    room = blocks * frame_count - taps
    later = sum(jnp.pad(products[s], ((0, 0), (s * wide, (room - s) * wide))) for s in range(frame_count))
    later = later.reshape(inputs_here, blocks, frame_count, wide)
    spectra = later[:, 0]
    for distance in range(1, blocks):
        spectra = spectra + from_behind(later[:, distance], "tm", distance)
    spectra = jnp.transpose(spectra, (1, 0, 2))
    spectra = (spectra * flags.astype(jnp.float32)[:, :, None]).astype(jnp.bfloat16)
    spectra = jnp.transpose(spectra.reshape(frame_count, inputs_here, 2, band_width), (0, 2, 3, 1))
    turned = lax.all_to_all(spectra, "tm", split_axis=2, concat_axis=0, tiled=True)
    return correlate(turned, lax.all_gather(turned, "inp", axis=3, tiled=True))


def solution(mesh):
    in_specs = (P(("grp", "tm"), "inp", None), P(), P(("grp", "tm"), "inp"))
    out_specs = P(("grp", "tm"), None, "inp", None)
    return jax.shard_map(shards, mesh=mesh, in_specs=in_specs, out_specs=out_specs, check_vma=False)
```

```python
import functools
import math

import jax
import jax.numpy as jnp
from jax import lax
from jax.experimental import pallas as pl
from jax.experimental.pallas import tpu as pltpu
from jax.sharding import PartitionSpec as P

NCH = 4096
CH_DEV = 2
STRIP = 1024
ROWS = 128


def channelize(tms, inps, fir_hbm, flags_ref, x_hbm, all_ref, fir_buf, x_buf, weights, total,
               part_out, part_in, flag_out, flag_in, fir_sem, x_sem, flag_sems, part_sems, all_sems):
    pieces, strips, frames, rows, strip = x_buf.shape
    taps, length = fir_buf.shape
    blocks = part_in.shape[2] // (2 * CH_DEV * frames)
    window = 2 * taps
    my_tm, my_inp = lax.axis_index("tm"), lax.axis_index("inp")

    def x_copy(piece, at):
        return pltpu.make_async_copy(
            x_hbm.at[:, pl.ds(piece * rows, rows), pl.ds(pl.multiple_of(at * strip, strip), strip)],
            x_buf.at[piece, at], x_sem.at[piece, at])

    def turn(axis, count, step):
        return {axis: lax.rem(lax.axis_index(axis) + step, count)}

    fir_copy = pltpu.make_async_copy(fir_hbm, fir_buf, fir_sem)
    fir_copy.start()
    for piece in range(pieces):
        for at in range(strips):
            x_copy(piece, at).start()

    barrier = pltpu.get_barrier_semaphore()
    for axis, count in (("tm", tms), ("inp", inps)):
        for step in range(1, count):
            pl.semaphore_signal(barrier, inc=1, device_id=turn(axis, count, step), device_id_type=pl.DeviceIdType.MESH)

    row = lax.broadcasted_iota(jnp.int32, (frames, frames), 0)
    col = lax.broadcasted_iota(jnp.int32, (frames, frames), 1)
    mirror = (row + col == frames - 1).astype(jnp.float32)
    mirrored = jnp.dot(mirror, flags_ref[...].astype(jnp.float32), preferred_element_type=jnp.float32)
    flag_out[...] = mirrored
    flag_in[my_tm] = mirrored

    group_count = tms * 2 * CH_DEV
    fir_copy.wait()

    def build(at, carry):
        group = lax.broadcasted_iota(jnp.int32, (group_count, strip), 0)
        sample = at * strip + lax.broadcasted_iota(jnp.int32, (group_count, strip), 1)
        slab = (group // (4 * CH_DEV)) * 2 + group % 2
        channel = NCH // 4 + slab * CH_DEV + (group // 4) % CH_DEV
        quarter = (group // 2) % 2
        phase = jnp.bitwise_and(sample * channel + quarter * (length // 4), length - 1)
        table = math.sqrt(2.0 / length) * jnp.cos((2.0 * math.pi / length) * phase.astype(jnp.float32))
        table = table.astype(jnp.bfloat16).astype(jnp.float32)
        fir = fir_buf[:, pl.ds(pl.multiple_of(at * strip, strip), strip)]
        for g in range(group_count):
            weights[at, g * taps:(g + 1) * taps, :] = (fir * table[g:g + 1, :]).astype(jnp.bfloat16)
        return carry

    lax.fori_loop(0, strips, build, 0)

    pl.semaphore_wait(barrier, tms + inps - 2)
    flag_copies = []
    for step in range(1, tms):
        copy = pltpu.make_async_remote_copy(
            flag_out, flag_in.at[my_tm], flag_sems.at[0, step - 1], flag_sems.at[1, step - 1],
            device_id=turn("tm", tms, step), device_id_type=pl.DeviceIdType.MESH)
        copy.start()
        flag_copies.append(copy)

    def multiply(piece, first, last):
        def step(at, carry):
            x_copy(piece, at).wait()
            voltages = x_buf[piece, at].reshape(frames * rows, strip)
            product = lax.dot_general(voltages, weights[at], (((1,), (1,)), ((), ())), preferred_element_type=jnp.float32)
            total[...] = jnp.where(at == 0, product, total[...] + product)
            return carry
        lax.fori_loop(first, last, step, 0)

    def send_parts(piece):
        lane = lax.broadcasted_iota(jnp.int32, (rows, 4 * CH_DEV * taps), 1)
        for slab in range(tms):
            pair, half = slab // 2, slab % 2
            kept = (lane // taps) % 2 == half
            at = slice(pair * 4 * CH_DEV * taps, (pair + 1) * 4 * CH_DEV * taps)
            value = None
            for s in range(frames):
                own = jnp.where(kept, total[s * rows:(s + 1) * rows, at], 0.0)
                value = own if value is None else value + own
                shift = 1 if s < frames - 1 or half == 0 else lane.shape[1] + 1 - taps
                value = pltpu.roll(value, shift, 1)
            turned = value.T
            ordered = [turned[q * window + (blocks - 1 - h) * frames:q * window + (blocks - h) * frames]
                       for h in range(blocks) for q in range(2 * CH_DEV)]
            part_out[piece, slab] = jnp.concatenate(ordered, axis=0).astype(jnp.bfloat16)
        part_in[piece, my_tm] = part_out[piece, my_tm]
        copies = []
        for step in range(1, tms):
            to = turn("tm", tms, step)
            copy = pltpu.make_async_remote_copy(
                part_out.at[piece, to["tm"]], part_in.at[piece, my_tm],
                part_sems.at[0, piece, step - 1], part_sems.at[1, piece, step - 1],
                device_id=to, device_id_type=pl.DeviceIdType.MESH)
            copy.start()
            copies.append(copy)
        return copies

    def gather(piece, part_copies):
        for copy in part_copies:
            copy.wait_recv()
        columns = slice(piece * rows, (piece + 1) * rows)
        per = 2 * CH_DEV * frames
        for block in range(tms):
            value = None
            for h in range(min(blocks, block + 1)):
                term = part_in[piece, block - h, h * per:(h + 1) * per, :].astype(jnp.float32)
                value = term if value is None else value + term
            good = flag_in[block, :, columns]
            value = value * jnp.concatenate([good] * (2 * CH_DEV), axis=0)
            all_ref[my_inp, block * per:(block + 1) * per, columns] = value.astype(jnp.bfloat16)
        copies = []
        for step in range(1, inps):
            copy = pltpu.make_async_remote_copy(
                all_ref.at[my_inp, :, columns], all_ref.at[my_inp, :, columns],
                all_sems.at[0, piece, step - 1], all_sems.at[1, piece, step - 1],
                device_id=turn("inp", inps, step), device_id_type=pl.DeviceIdType.MESH)
            copy.start()
            copies.append(copy)
        return copies

    waiting, before = list(flag_copies), None
    for piece in range(pieces):
        middle = strips // 2 if before is not None else 0
        multiply(piece, 0, middle)
        if before is not None:
            if piece == 1:
                for copy in flag_copies:
                    copy.wait_recv()
            waiting += before
            got = gather(piece - 1, before)
            waiting += got
        multiply(piece, middle, strips)
        before = send_parts(piece)
    if pieces == 1:
        for copy in flag_copies:
            copy.wait_recv()
    waiting += before
    waiting += gather(pieces - 1, before)
    gathers = [copy for copy in waiting]
    for copy in gathers:
        copy.wait_send()
    return [copy for copy in waiting]


def channelize_body(tms, inps, *refs):
    pieces = refs[5].shape[0]
    waiting = channelize(tms, inps, *refs)
    flag_count, part_count, all_count = tms - 1, tms - 1, inps - 1
    at = flag_count
    for piece in range(pieces):
        at += part_count
        for copy in waiting[at:at + all_count]:
            copy.wait_recv()
        at += all_count


def correlate(inps, scale, all_ref, out_ref, sides):
    channel, part = pl.program_id(0), pl.program_id(1)
    rows = all_ref.shape[2]
    lane = lax.broadcasted_iota(jnp.int32, sides.shape[1:], 1)
    per = sides.shape[2] // scale[1]

    @pl.when(jnp.logical_and(channel == 0, part == 0))
    def _():
        own = all_ref[lax.axis_index("inp")].astype(jnp.float32).T
        size = own.shape[1]
        sides[0] = own
        sides[1] = jnp.where((lane // per) % 2 == 0, pltpu.roll(own, size - per, 1), -pltpu.roll(own, per, 1))

    side = jnp.where((lane // (2 * per)) % CH_DEV == channel, sides[part], 0.0).astype(jnp.bfloat16)
    for peer in range(inps):
        value = jnp.dot(side, all_ref[peer], preferred_element_type=jnp.float32)
        out_ref[0, 0, :, peer * rows:(peer + 1) * rows] = value * scale[0]


def shards(samples, fir, flags):
    frames, inputs, length = samples.shape
    taps = fir.shape[0]
    tms, inps = lax.axis_size("tm"), lax.axis_size("inp")
    blocks = (taps + frames - 2) // frames + 1
    assert length & (length - 1) == 0 and tms % 2 == 0 and blocks * frames <= 2 * taps
    rows = min(inputs, ROWS)
    pieces, strips = inputs // rows, length // STRIP
    columns = tms * 2 * CH_DEV * taps
    per = 2 * CH_DEV * frames
    vmem = pl.BlockSpec(memory_space=pltpu.VMEM)
    anywhere = pl.BlockSpec(memory_space=pl.ANY)
    every = pl.pallas_call(
        functools.partial(channelize_body, tms, inps),
        out_shape=jax.ShapeDtypeStruct((inps, tms * per, inputs), jnp.bfloat16),
        in_specs=[anywhere, vmem, anywhere],
        out_specs=vmem,
        scratch_shapes=[
            pltpu.VMEM((taps, length), jnp.float32),
            pltpu.VMEM((pieces, strips, frames, rows, STRIP), jnp.bfloat16),
            pltpu.VMEM((strips, columns, STRIP), jnp.bfloat16),
            pltpu.VMEM((frames * rows, columns), jnp.float32),
            pltpu.VMEM((pieces, tms, blocks * per, rows), jnp.bfloat16),
            pltpu.VMEM((pieces, tms, blocks * per, rows), jnp.bfloat16),
            pltpu.VMEM((frames, inputs), jnp.float32),
            pltpu.VMEM((tms, frames, inputs), jnp.float32),
            pltpu.SemaphoreType.DMA,
            pltpu.SemaphoreType.DMA((pieces, strips)),
            pltpu.SemaphoreType.DMA((2, tms - 1)),
            pltpu.SemaphoreType.DMA((2, pieces, tms - 1)),
            pltpu.SemaphoreType.DMA((2, pieces, inps - 1)),
        ],
        compiler_params=pltpu.CompilerParams(collective_id=0, has_side_effects=True, vmem_limit_bytes=60 << 20),
        name="channelize",
    )(fir, flags, samples)
    return pl.pallas_call(
        functools.partial(correlate, inps, (1.0 / (frames * tms), 2 * CH_DEV * tms)),
        out_shape=jax.ShapeDtypeStruct((CH_DEV, 2, inputs, inps * inputs), jnp.float32),
        grid=(CH_DEV, 2),
        in_specs=[pl.BlockSpec((inps, tms * per, inputs), lambda c, p: (0, 0, 0))],
        out_specs=pl.BlockSpec((1, 1, inputs, inps * inputs), lambda c, p: (c, p, 0, 0)),
        scratch_shapes=[pltpu.VMEM((2, inputs, tms * per), jnp.float32)],
        name="correlate",
    )(every)


def solution(mesh):
    in_specs = (P(("grp", "tm"), "inp", None), P(), P(("grp", "tm"), "inp"))
    out_specs = P(("grp", "tm"), None, "inp", None)
    return jax.shard_map(shards, mesh=mesh, in_specs=in_specs, out_specs=out_specs, check_vma=False)
```

```python
import functools
import math

import jax
import jax.numpy as jnp
from jax import lax
from jax.experimental import pallas as pl
from jax.experimental.pallas import tpu as pltpu
from jax.sharding import PartitionSpec as P

NCH = 4096
CH_DEV = 2
STRIP = 1024
ROWS = 128


def channelize(tms, inps, fir_hbm, flags_ref, x_hbm, all_ref, fir_buf, x_buf, weights, total,
               part_out, part_in, flag_out, flag_in, turns, fir_sem, x_sem, flag_sems, part_sems, all_sems):
    pieces, strips, frames, rows, strip = x_buf.shape
    taps, length = fir_buf.shape
    blocks = part_in.shape[2] // (2 * CH_DEV * frames)
    window = 2 * taps
    my_tm, my_inp = lax.axis_index("tm"), lax.axis_index("inp")

    def x_copy(piece, at):
        return pltpu.make_async_copy(
            x_hbm.at[:, pl.ds(piece * rows, rows), pl.ds(pl.multiple_of(at * strip, strip), strip)],
            x_buf.at[piece, at], x_sem.at[piece, at])

    def turn(axis, count, step):
        return {axis: lax.rem(lax.axis_index(axis) + step, count)}

    fir_copy = pltpu.make_async_copy(fir_hbm, fir_buf, fir_sem)
    fir_copy.start()
    for piece in range(pieces):
        for at in range(strips):
            x_copy(piece, at).start()

    barrier = pltpu.get_barrier_semaphore()
    for axis, count in (("tm", tms), ("inp", inps)):
        for step in range(1, count):
            pl.semaphore_signal(barrier, inc=1, device_id=turn(axis, count, step), device_id_type=pl.DeviceIdType.MESH)

    row = lax.broadcasted_iota(jnp.int32, (frames, frames), 0)
    col = lax.broadcasted_iota(jnp.int32, (frames, frames), 1)
    mirror = (row + col == frames - 1).astype(jnp.float32)
    mirrored = jnp.dot(mirror, flags_ref[...].astype(jnp.float32), preferred_element_type=jnp.float32)
    flag_out[...] = mirrored
    flag_in[my_tm] = mirrored

    group_count = tms * 2 * CH_DEV

    def channel_of(shape):
        group = lax.broadcasted_iota(jnp.int32, shape, 0)
        slab = (group // (4 * CH_DEV)) * 2 + group % 2
        return NCH // 4 + slab * CH_DEV + (group // 4) % CH_DEV, (group // 2) % 2

    def cosine(phase):
        return jnp.cos((2.0 * math.pi / length) * jnp.bitwise_and(phase, length - 1).astype(jnp.float32))

    channel, quarter = channel_of((group_count, strip))
    phase = lax.broadcasted_iota(jnp.int32, (group_count, strip), 1) * channel + quarter * (length // 4)
    factor = math.sqrt(2.0 / length)
    turns[0] = factor * cosine(phase)
    turns[1] = factor * cosine(phase - length // 4)
    channel, _ = channel_of((group_count, 128))
    step_phase = lax.broadcasted_iota(jnp.int32, (group_count, 128), 1) * strip * channel
    turn_cos, turn_sin = cosine(step_phase), cosine(step_phase - length // 4)
    fir_copy.wait()

    for at in range(strips):
        table = turns[0] * turn_cos[:, at:at + 1] - turns[1] * turn_sin[:, at:at + 1]
        table = table.astype(jnp.bfloat16).astype(jnp.float32)
        fir = fir_buf[:, at * strip:(at + 1) * strip]
        for g in range(group_count):
            weights[at, g * taps:(g + 1) * taps, :] = (fir * table[g:g + 1, :]).astype(jnp.bfloat16)

    def send_flags():
        pl.semaphore_wait(barrier, tms + inps - 2)
        copies = []
        for step in range(1, tms):
            copy = pltpu.make_async_remote_copy(
                flag_out, flag_in.at[my_tm], flag_sems.at[0, step - 1], flag_sems.at[1, step - 1],
                device_id=turn("tm", tms, step), device_id_type=pl.DeviceIdType.MESH)
            copy.start()
            copies.append(copy)
        return copies

    def multiply(piece):
        def add(at, carry):
            x_copy(piece, at).wait()
            voltages = x_buf[piece, at].reshape(frames * rows, strip)
            product = lax.dot_general(voltages, weights[at], (((1,), (1,)), ((), ())), preferred_element_type=jnp.float32)
            total[...] = jnp.where(at == 0, product, total[...] + product)
            return carry
        lax.fori_loop(0, strips, add, 0)

    def part_copy(piece, slot, to):
        return pltpu.make_async_remote_copy(
            part_out.at[piece, to], part_in.at[piece, slot], part_sems.at[0, piece, to], part_sems.at[1, piece, slot],
            device_id={"tm": to}, device_id_type=pl.DeviceIdType.MESH)

    def send_parts(piece):
        wide, room, pairs = 4 * CH_DEV * taps, blocks * frames - taps, tms // 2
        place = lax.broadcasted_iota(jnp.int32, (rows, wide), 1) % window
        my_pair, my_half = my_tm // 2, lax.rem(my_tm, 2)
        for ahead in range(1, pairs + 1):
            pair = lax.rem(my_pair + ahead, pairs)
            lanes = pl.ds(pl.multiple_of(pair * wide, wide), wide)
            first = second = None
            for s in range(frames):
                moved = pltpu.roll(total[s * rows:(s + 1) * rows, lanes], room - s, 1)
                inside = jnp.logical_and(place >= room - s, place < room - s + taps)
                one, two = jnp.where(inside, moved, 0.0), jnp.where(inside, 0.0, moved)
                first, second = (one, two) if s == 0 else (first + one, second + two)
            for half, value in enumerate((first, pltpu.roll(second, wide - taps, 1))):
                turned = value.T
                ordered = [turned[q * window + (blocks - 1 - h) * frames:q * window + (blocks - h) * frames]
                           for h in range(blocks) for q in range(2 * CH_DEV)]
                part_out[piece, 2 * pair + half] = jnp.concatenate(ordered, axis=0).astype(jnp.bfloat16)
                if ahead < pairs:
                    part_copy(piece, my_tm, 2 * pair + half).start()
        part_copy(piece, my_tm, 2 * my_pair + 1 - my_half).start()
        part_in[piece, my_tm] = part_out[piece, my_tm]

    def gather(piece):
        for step in range(1, tms):
            source = lax.rem(my_tm + step, tms)
            part_copy(piece, source, source).wait_recv()
        columns = slice(piece * rows, (piece + 1) * rows)
        per = 2 * CH_DEV * frames
        for block in range(tms):
            value = None
            for h in range(min(blocks, block + 1)):
                term = part_in[piece, block - h, h * per:(h + 1) * per, :].astype(jnp.float32)
                value = term if value is None else value + term
            good = flag_in[block, :, columns]
            value = value * jnp.concatenate([good] * (2 * CH_DEV), axis=0)
            all_ref[my_inp, block * per:(block + 1) * per, columns] = value.astype(jnp.bfloat16)
        copies = []
        for step in range(1, inps):
            copy = pltpu.make_async_remote_copy(
                all_ref.at[my_inp, :, columns], all_ref.at[my_inp, :, columns],
                all_sems.at[0, piece, step - 1], all_sems.at[1, piece, step - 1],
                device_id=turn("inp", inps, step), device_id_type=pl.DeviceIdType.MESH)
            copy.start()
            copies.append(copy)
        return copies

    flag_copies, all_copies = [], []

    def gather_after(piece):
        if piece == 0:
            for copy in flag_copies:
                copy.wait_recv()
        all_copies.extend(gather(piece))

    for piece in range(pieces):
        multiply(piece)
        if piece == 0:
            flag_copies.extend(send_flags())
        send_parts(piece)
        if piece > 0:
            gather_after(piece - 1)
    gather_after(pieces - 1)
    for copy in all_copies:
        copy.wait_recv()
    for copy in flag_copies + all_copies:
        copy.wait_send()
    for piece in range(pieces):
        for step in range(1, tms):
            to = lax.rem(my_tm + step, tms)
            part_copy(piece, my_tm, to).wait_send()


def correlate(inps, scale, all_ref, out_ref, sides, stage, sems):
    rows = all_ref.shape[2]
    own = all_ref[lax.axis_index("inp")].astype(jnp.float32).T * scale[0]
    size = own.shape[1]
    per = size // scale[1]
    lane = lax.broadcasted_iota(jnp.int32, own.shape, 1)
    sides[0] = own
    sides[1] = jnp.where((lane // per) % 2 == 0, pltpu.roll(own, size - per, 1), -pltpu.roll(own, per, 1))
    copies = []
    for channel in range(CH_DEV):
        for part in range(2):
            side = jnp.where((lane // (2 * per)) % CH_DEV == channel, sides[part], 0.0).astype(jnp.bfloat16)
            for peer in range(inps):
                columns = slice(peer * rows, (peer + 1) * rows)
                stage[channel, part, :, columns] = jnp.dot(side, all_ref[peer], preferred_element_type=jnp.float32)
            copy = pltpu.make_async_copy(stage.at[channel, part], out_ref.at[channel, part], sems.at[channel, part])
            copy.start()
            copies.append(copy)
    for copy in copies:
        copy.wait()


def shards(samples, fir, flags):
    frames, inputs, length = samples.shape
    taps = fir.shape[0]
    tms, inps = lax.axis_size("tm"), lax.axis_size("inp")
    blocks = (taps + frames - 2) // frames + 1
    assert length // STRIP <= 128 and length & (length - 1) == 0 and tms % 2 == 0 and blocks * frames <= 2 * taps
    rows = min(inputs, ROWS)
    pieces, strips = inputs // rows, length // STRIP
    columns = tms * 2 * CH_DEV * taps
    per = 2 * CH_DEV * frames
    vmem = pl.BlockSpec(memory_space=pltpu.VMEM)
    anywhere = pl.BlockSpec(memory_space=pl.ANY)
    every = pl.pallas_call(
        functools.partial(channelize, tms, inps),
        out_shape=jax.ShapeDtypeStruct((inps, tms * per, inputs), jnp.bfloat16),
        in_specs=[anywhere, vmem, anywhere],
        out_specs=vmem,
        scratch_shapes=[
            pltpu.VMEM((taps, length), jnp.float32),
            pltpu.VMEM((pieces, strips, frames, rows, STRIP), jnp.bfloat16),
            pltpu.VMEM((strips, columns, STRIP), jnp.bfloat16),
            pltpu.VMEM((frames * rows, columns), jnp.float32),
            pltpu.VMEM((pieces, tms, blocks * per, rows), jnp.bfloat16),
            pltpu.VMEM((pieces, tms, blocks * per, rows), jnp.bfloat16),
            pltpu.VMEM((frames, inputs), jnp.float32),
            pltpu.VMEM((tms, frames, inputs), jnp.float32),
            pltpu.VMEM((2, tms * 2 * CH_DEV, STRIP), jnp.float32),
            pltpu.SemaphoreType.DMA,
            pltpu.SemaphoreType.DMA((pieces, strips)),
            pltpu.SemaphoreType.DMA((2, tms - 1)),
            pltpu.SemaphoreType.DMA((2, pieces, tms)),
            pltpu.SemaphoreType.DMA((2, pieces, inps - 1)),
        ],
        compiler_params=pltpu.CompilerParams(collective_id=0, has_side_effects=True, vmem_limit_bytes=60 << 20),
        name="channelize",
    )(fir, flags, samples)
    return pl.pallas_call(
        functools.partial(correlate, inps, (1.0 / (frames * tms), 2 * CH_DEV * tms)),
        out_shape=jax.ShapeDtypeStruct((CH_DEV, 2, inputs, inps * inputs), jnp.float32),
        in_specs=[vmem],
        out_specs=anywhere,
        scratch_shapes=[
            pltpu.VMEM((2, inputs, tms * per), jnp.float32),
            pltpu.VMEM((CH_DEV, 2, inputs, inps * inputs), jnp.float32),
            pltpu.SemaphoreType.DMA((CH_DEV, 2)),
        ],
        name="correlate",
    )(every)


def solution(mesh):
    in_specs = (P(("grp", "tm"), "inp", None), P(), P(("grp", "tm"), "inp"))
    out_specs = P(("grp", "tm"), None, "inp", None)
    return jax.shard_map(shards, mesh=mesh, in_specs=in_specs, out_specs=out_specs, check_vma=False)
```

```python
import functools
import math

import jax
import jax.numpy as jnp
from jax import lax
from jax.experimental import pallas as pl
from jax.experimental.pallas import tpu as pltpu
from jax.sharding import PartitionSpec as P

NCH = 4096
CH_DEV = 2
STRIP = 2048
ROWS = 128


def channelize(tms, inps, fir_hbm, flags_ref, x_hbm, all_ref, fir_buf, x_buf, weights, total,
               part_out, part_in, flag_out, flag_in, turns, fir_sem, x_sem, flag_sems, part_sems, all_sems):
    pieces, strips, frames, rows, strip = x_buf.shape
    taps, length = fir_buf.shape
    blocks = part_in.shape[2] // (2 * CH_DEV * frames)
    window = 2 * taps
    my_tm, my_inp = lax.axis_index("tm"), lax.axis_index("inp")

    def x_copy(piece, at):
        return pltpu.make_async_copy(
            x_hbm.at[:, pl.ds(piece * rows, rows), pl.ds(pl.multiple_of(at * strip, strip), strip)],
            x_buf.at[piece, at], x_sem.at[piece, at])

    def turn(axis, count, step):
        return {axis: lax.rem(lax.axis_index(axis) + step, count)}

    fir_copy = pltpu.make_async_copy(fir_hbm, fir_buf, fir_sem)
    fir_copy.start()
    for piece in range(pieces):
        for at in range(strips):
            x_copy(piece, at).start()

    barrier = pltpu.get_barrier_semaphore()
    for axis, count in (("tm", tms), ("inp", inps)):
        for step in range(1, count):
            pl.semaphore_signal(barrier, inc=1, device_id=turn(axis, count, step), device_id_type=pl.DeviceIdType.MESH)

    row = lax.broadcasted_iota(jnp.int32, (frames, frames), 0)
    col = lax.broadcasted_iota(jnp.int32, (frames, frames), 1)
    mirror = (row + col == frames - 1).astype(jnp.float32)
    mirrored = jnp.dot(mirror, flags_ref[...].astype(jnp.float32), preferred_element_type=jnp.float32)
    flag_out[...] = mirrored
    flag_in[my_tm] = mirrored

    group_count = tms * 2 * CH_DEV

    def channel_of(shape):
        group = lax.broadcasted_iota(jnp.int32, shape, 0)
        slab = (group // (4 * CH_DEV)) * 2 + group % 2
        return NCH // 4 + slab * CH_DEV + (group // 4) % CH_DEV, (group // 2) % 2

    def cosine(phase):
        return jnp.cos((2.0 * math.pi / length) * jnp.bitwise_and(phase, length - 1).astype(jnp.float32))

    channel, quarter = channel_of((group_count, strip))
    phase = lax.broadcasted_iota(jnp.int32, (group_count, strip), 1) * channel + quarter * (length // 4)
    factor = math.sqrt(2.0 / length)
    turns[0] = factor * cosine(phase)
    turns[1] = factor * cosine(phase - length // 4)
    channel, _ = channel_of((group_count, 128))
    step_phase = lax.broadcasted_iota(jnp.int32, (group_count, 128), 1) * strip * channel
    turn_cos, turn_sin = cosine(step_phase), cosine(step_phase - length // 4)
    fir_copy.wait()

    for at in range(strips):
        table = turns[0] * turn_cos[:, at:at + 1] - turns[1] * turn_sin[:, at:at + 1]
        table = table.astype(jnp.bfloat16).astype(jnp.float32)
        fir = fir_buf[:, at * strip:(at + 1) * strip]
        for g in range(group_count):
            weights[at, g * taps:(g + 1) * taps, :] = (fir * table[g:g + 1, :]).astype(jnp.bfloat16)

    def send_flags():
        pl.semaphore_wait(barrier, tms + inps - 2)
        copies = []
        for step in range(1, tms):
            copy = pltpu.make_async_remote_copy(
                flag_out, flag_in.at[my_tm], flag_sems.at[0, step - 1], flag_sems.at[1, step - 1],
                device_id=turn("tm", tms, step), device_id_type=pl.DeviceIdType.MESH)
            copy.start()
            copies.append(copy)
        return copies

    def multiply(piece):
        def add(at, carry):
            x_copy(piece, at).wait()
            voltages = x_buf[piece, at].reshape(frames * rows, strip)
            product = lax.dot_general(voltages, weights[at], (((1,), (1,)), ((), ())), preferred_element_type=jnp.float32)
            total[...] = jnp.where(at == 0, product, total[...] + product)
            return carry
        lax.fori_loop(0, strips, add, 0)

    def part_copy(piece, slot, to):
        return pltpu.make_async_remote_copy(
            part_out.at[piece, to], part_in.at[piece, slot], part_sems.at[0, piece, to], part_sems.at[1, piece, slot],
            device_id={"tm": to}, device_id_type=pl.DeviceIdType.MESH)

    def send_parts(piece):
        wide, room, pairs = 4 * CH_DEV * taps, blocks * frames - taps, tms // 2
        place = lax.broadcasted_iota(jnp.int32, (rows, wide), 1) % window
        my_pair, my_half = my_tm // 2, lax.rem(my_tm, 2)
        for ahead in range(1, pairs + 1):
            pair = lax.rem(my_pair + ahead, pairs)
            lanes = pl.ds(pl.multiple_of(pair * wide, wide), wide)
            first = second = None
            for s in range(frames):
                moved = pltpu.roll(total[s * rows:(s + 1) * rows, lanes], room - s, 1)
                inside = jnp.logical_and(place >= room - s, place < room - s + taps)
                one, two = jnp.where(inside, moved, 0.0), jnp.where(inside, 0.0, moved)
                first, second = (one, two) if s == 0 else (first + one, second + two)
            for half, value in enumerate((first, pltpu.roll(second, wide - taps, 1))):
                turned = value.T
                ordered = [turned[q * window + (blocks - 1 - h) * frames:q * window + (blocks - h) * frames]
                           for h in range(blocks) for q in range(2 * CH_DEV)]
                part_out[piece, 2 * pair + half] = jnp.concatenate(ordered, axis=0).astype(jnp.bfloat16)
                if ahead < pairs:
                    part_copy(piece, my_tm, 2 * pair + half).start()
        part_copy(piece, my_tm, 2 * my_pair + 1 - my_half).start()
        part_in[piece, my_tm] = part_out[piece, my_tm]

    def gather(piece):
        for step in range(1, tms):
            source = lax.rem(my_tm + step, tms)
            part_copy(piece, source, source).wait_recv()
        columns = slice(piece * rows, (piece + 1) * rows)
        per = 2 * CH_DEV * frames
        for block in range(tms):
            value = None
            for h in range(min(blocks, block + 1)):
                term = part_in[piece, block - h, h * per:(h + 1) * per, :].astype(jnp.float32)
                value = term if value is None else value + term
            good = flag_in[block, :, columns]
            value = value * jnp.concatenate([good] * (2 * CH_DEV), axis=0)
            all_ref[my_inp, block * per:(block + 1) * per, columns] = value.astype(jnp.bfloat16)
        copies = []
        for step in range(1, inps):
            copy = pltpu.make_async_remote_copy(
                all_ref.at[my_inp, :, columns], all_ref.at[my_inp, :, columns],
                all_sems.at[0, piece, step - 1], all_sems.at[1, piece, step - 1],
                device_id=turn("inp", inps, step), device_id_type=pl.DeviceIdType.MESH)
            copy.start()
            copies.append(copy)
        return copies

    flag_copies, all_copies = [], []

    def gather_after(piece):
        if piece == 0:
            for copy in flag_copies:
                copy.wait_recv()
        all_copies.extend(gather(piece))

    for piece in range(pieces):
        multiply(piece)
        if piece == 0:
            flag_copies.extend(send_flags())
        send_parts(piece)
        if piece > 0:
            gather_after(piece - 1)
    gather_after(pieces - 1)
    for copy in all_copies:
        copy.wait_recv()
    for copy in flag_copies + all_copies:
        copy.wait_send()
    for piece in range(pieces):
        for step in range(1, tms):
            to = lax.rem(my_tm + step, tms)
            part_copy(piece, my_tm, to).wait_send()


def correlate(inps, scale, all_ref, out_ref, sides, stage, sems):
    rows = all_ref.shape[2]
    own = all_ref[lax.axis_index("inp")].astype(jnp.float32).T * scale[0]
    size = own.shape[1]
    per = size // scale[1]
    lane = lax.broadcasted_iota(jnp.int32, own.shape, 1)
    sides[0] = own
    sides[1] = jnp.where((lane // per) % 2 == 0, pltpu.roll(own, size - per, 1), -pltpu.roll(own, per, 1))
    copies = []
    for channel in range(CH_DEV):
        for part in range(2):
            side = jnp.where((lane // (2 * per)) % CH_DEV == channel, sides[part], 0.0).astype(jnp.bfloat16)
            for peer in range(inps):
                columns = slice(peer * rows, (peer + 1) * rows)
                stage[channel, part, :, columns] = jnp.dot(side, all_ref[peer], preferred_element_type=jnp.float32)
            copy = pltpu.make_async_copy(stage.at[channel, part], out_ref.at[channel, part], sems.at[channel, part])
            copy.start()
            copies.append(copy)
    for copy in copies:
        copy.wait()


def shards(samples, fir, flags):
    frames, inputs, length = samples.shape
    taps = fir.shape[0]
    tms, inps = lax.axis_size("tm"), lax.axis_size("inp")
    blocks = (taps + frames - 2) // frames + 1
    assert length // STRIP <= 128 and length & (length - 1) == 0 and tms % 2 == 0 and blocks * frames <= 2 * taps
    rows = min(inputs, ROWS)
    pieces, strips = inputs // rows, length // STRIP
    columns = tms * 2 * CH_DEV * taps
    per = 2 * CH_DEV * frames
    vmem = pl.BlockSpec(memory_space=pltpu.VMEM)
    anywhere = pl.BlockSpec(memory_space=pl.ANY)
    every = pl.pallas_call(
        functools.partial(channelize, tms, inps),
        out_shape=jax.ShapeDtypeStruct((inps, tms * per, inputs), jnp.bfloat16),
        in_specs=[anywhere, vmem, anywhere],
        out_specs=vmem,
        scratch_shapes=[
            pltpu.VMEM((taps, length), jnp.float32),
            pltpu.VMEM((pieces, strips, frames, rows, STRIP), jnp.bfloat16),
            pltpu.VMEM((strips, columns, STRIP), jnp.bfloat16),
            pltpu.VMEM((frames * rows, columns), jnp.float32),
            pltpu.VMEM((pieces, tms, blocks * per, rows), jnp.bfloat16),
            pltpu.VMEM((pieces, tms, blocks * per, rows), jnp.bfloat16),
            pltpu.VMEM((frames, inputs), jnp.float32),
            pltpu.VMEM((tms, frames, inputs), jnp.float32),
            pltpu.VMEM((2, tms * 2 * CH_DEV, STRIP), jnp.float32),
            pltpu.SemaphoreType.DMA,
            pltpu.SemaphoreType.DMA((pieces, strips)),
            pltpu.SemaphoreType.DMA((2, tms - 1)),
            pltpu.SemaphoreType.DMA((2, pieces, tms)),
            pltpu.SemaphoreType.DMA((2, pieces, inps - 1)),
        ],
        compiler_params=pltpu.CompilerParams(collective_id=0, has_side_effects=True, vmem_limit_bytes=60 << 20),
        name="channelize",
    )(fir, flags, samples)
    return pl.pallas_call(
        functools.partial(correlate, inps, (1.0 / (frames * tms), 2 * CH_DEV * tms)),
        out_shape=jax.ShapeDtypeStruct((CH_DEV, 2, inputs, inps * inputs), jnp.float32),
        in_specs=[vmem],
        out_specs=anywhere,
        scratch_shapes=[
            pltpu.VMEM((2, inputs, tms * per), jnp.float32),
            pltpu.VMEM((CH_DEV, 2, inputs, inps * inputs), jnp.float32),
            pltpu.SemaphoreType.DMA((CH_DEV, 2)),
        ],
        name="correlate",
    )(every)


def solution(mesh):
    in_specs = (P(("grp", "tm"), "inp", None), P(), P(("grp", "tm"), "inp"))
    out_specs = P(("grp", "tm"), None, "inp", None)
    return jax.shard_map(shards, mesh=mesh, in_specs=in_specs, out_specs=out_specs, check_vma=False)
```
